32 devices in a mesh: band: 16 (over z, y, core), pw: 2 (over x).
Axes of the slice: x: 2, y: 2, z: 4, core: 2. Of those that a mesh axis runs over, the one named last changes fastest.
Arguments:
- mel: bfloat16 [32, 256, 32768], P('band', None, 'pw'), may hold values from -6 to 6
- pole_amp: bfloat16 [32768, 256], P('pw', 'band'), may hold values from 0.19921875 to 5
- pole_freq: bfloat16 [32768, 256], P('pw', 'band'), may hold values from 0.5 to 4
- band_energy: float32 [32], P('band'), may hold values from -3 to 3
- occupation: int32 [32], P('band'), may hold values from 0 to 1
- column_map: int32 [256], replicated, may hold values from 0 to 32767
- energies: float32 [2], replicated, may hold values from -2 to 2
Outputs:
- sigma: float32 [2, 256, 256], P(None, 'pw')
The draws below stay inside these ranges and needn't reach their ends.
All inputs are finite; a program needn't handle non-finite values.
Results may differ from the reference program's by a relative error of at most 0.0055.
Values may be sent and summed in bfloat16 or wider, within the bound.
No kernel may reach another device: no remote copies, remote signals or barrier semaphores. Data moves between devices by JAX's collectives and lax.ppermute only.
A program may use at most 64 MiB of HBM per device.

```python
import math
import jax
import jax.numpy as jnp
from jax import lax

NG = 32768
NC = 256
NS = 256
NE = 2
NB = 32


def plant(entries, key, low, top_value):
    dims = entries.shape
    index_at = [jax.random.randint(jax.random.fold_in(key, axis), (), 0, dims[axis]) for axis in range(len(dims))]
    entries = entries.at[tuple(index_at)].set(low)
    longest = dims.index(max(dims))
    index_at[longest] = (index_at[longest] + 1) % dims[longest]
    return entries.at[tuple(index_at)].set(top_value)


def levels(key, extent, shards, low, largest):
    loudness, own = 1.0, jax.random.fold_in(key, 6)
    for position, blocks in shards:
        steps = jnp.exp(jax.random.uniform(jax.random.fold_in(own, position), (blocks,), jnp.float32, low / len(shards), largest / len(shards)))
        loudness = loudness * jnp.repeat(steps, extent[position] // blocks).reshape([-1 if axis == position else 1 for axis in range(len(extent))])
    return loudness


def normal_values(key, extent, spread, limit, cuts=(), held_as=jnp.bfloat16):
    drawn = spread * jax.random.normal(key, extent, jnp.float32)
    if cuts:
        drawn = drawn * levels(key, extent, cuts, -0.22, 0.18)
    return jnp.clip(drawn, -limit, limit).astype(held_as)


def setup_inputs(seed: int = 0) -> dict:
    arg_keys = jax.random.split(jax.random.key(seed), 8)
    return {
        "mel": normal_values(arg_keys[0], (NB, NS, NG), 1.0, 6.0, ((0, 16), (2, 2))),
        "pole_amp": jnp.clip(jnp.exp(math.log(5.0) - 3.2227897 * jax.random.uniform(arg_keys[1], (NG, NC), jnp.float32) ** levels(arg_keys[1], (NG, NC), ((0, 2), (1, 16)), -0.2, 0.2)), 0.19921875, 5.0).astype(jnp.bfloat16),
        "pole_freq": jnp.clip(jnp.exp(math.log(4.0) - 2.0794415 * jax.random.uniform(arg_keys[2], (NG, NC), jnp.float32) ** levels(arg_keys[2], (NG, NC), ((0, 2), (1, 16)), -0.2, 0.2)), 0.5, 4.0).astype(jnp.bfloat16),
        "band_energy": jnp.clip(jax.random.uniform(arg_keys[3], (NB,), jnp.float32, -3.0, 3.0) * levels(arg_keys[3], (NB,), ((0, 16),), -0.4, 0.0), -3.0, 3.0),
        "occupation": plant(jax.random.randint(arg_keys[4], (NB,), 0, 2), jax.random.fold_in(arg_keys[4], 1), 0, 1).astype(jnp.int32),
        "column_map": plant(jax.random.randint(arg_keys[5], (NC,), 0, NG), jax.random.fold_in(arg_keys[5], 1), 0, NG - 1).astype(jnp.int32),
        "energies": jnp.clip(jax.random.uniform(arg_keys[6], (NE,), jnp.float32, -2.0, 2.0), -2.0, 2.0),
    }


broadening = 0.4

def reference(mel, pole_amp, pole_freq, band_energy, occupation, column_map, energies):
    chosen = jnp.take(mel, column_map.astype(jnp.int32), axis=2)
    amplitude = pole_amp.astype(jnp.float32)
    frequency = pole_freq.astype(jnp.float32)
    strength = amplitude / frequency
    branch_sign = (2 * occupation - 1).astype(jnp.float32)

    def one_band(summed, slices):
        elements, picked, band_level, side_sign = slices
        results = []
        for energy_index in range(NE):
            offset_gap = energies[energy_index] - band_level + side_sign * frequency
            screened = (strength * offset_gap / (offset_gap * offset_gap + broadening * broadening)).astype(jnp.bfloat16)
            contracted = jnp.dot(elements, screened, preferred_element_type=jnp.float32)
            results.append(jnp.dot(contracted, picked.astype(jnp.float32).T, precision=lax.Precision.HIGHEST))
        return (summed + jnp.stack(results), None)
    start_value = jnp.zeros((NE, NS, NS), jnp.float32)
    summed, _ = lax.scan(one_band, start_value, (mel, chosen, band_energy, branch_sign))
    return summed / math.sqrt(NG * NC * NB)
```

```python
import functools
import math

import jax
import jax.numpy as jnp
from jax import lax
from jax.experimental import pallas as pl
from jax.experimental.pallas import tpu as pltpu
from jax.sharding import PartitionSpec as P

broadening = 0.4
LANES = 128
VM = pltpu.VMEM


contract_minor = (((1,), (1,)), ((), ()))


def swap(value, axis, size, mask):
    return lax.ppermute(value, axis, [(i, i ^ mask) for i in range(size)])


def largest_block(extent, limit):
    block = extent
    while block > limit and block % (2 * LANES) == 0:
        block //= 2
    return block


def pick_kernel(sign_ref, index_ref, mel_ref, out_ref, acc_ref):
    step = pl.program_id(0)
    bands, _, width = mel_ref.shape
    columns = index_ref.shape[0]
    lane = lax.broadcasted_iota(jnp.int32, (columns, width), 1) + step * width
    hot = (lane == index_ref[...]).astype(jnp.float32).astype(jnp.bfloat16)

    @pl.when(step == 0)
    def _():
        acc_ref[...] = jnp.zeros_like(acc_ref)

    for m in range(bands):
        acc_ref[m] += lax.dot_general(
            hot, mel_ref[m], contract_minor, preferred_element_type=jnp.float32
        )

    @pl.when(step == pl.num_programs(0) - 1)
    def _():
        for m in range(bands):
            out_ref[m] = (acc_ref[m] * sign_ref[m]).astype(out_ref.dtype)


def pick(mel, index, sign):
    bands, states, rows = mel.shape
    columns = index.shape[0]
    width = largest_block(rows, 1024)
    return pl.pallas_call(
        pick_kernel,
        grid=(rows // width,),
        in_specs=[
            pl.BlockSpec(memory_space=pltpu.SMEM),
            pl.BlockSpec((columns, 1), lambda i: (0, 0)),
            pl.BlockSpec((bands, states, width), lambda i: (0, 0, i)),
        ],
        out_specs=pl.BlockSpec((bands, columns, states), lambda i: (0, 0, 0)),
        out_shape=jax.ShapeDtypeStruct((bands, columns, states), jnp.bfloat16),
        scratch_shapes=[VM((bands, columns, states), jnp.float32)],
        cost_estimate=pl.CostEstimate(
            flops=2 * bands * columns * states * rows,
            bytes_accessed=2 * mel.size,
            transcendentals=0,
        ),
        name="pick",
    )(sign, index.reshape(columns, 1), mel)


def screened_block(shift, amplitude, frequency):
    gap = [frequency + s for s in shift]
    level = [[h * h + broadening * broadening for h in gap]]
    while len(level[-1]) > 1:
        row = level[-1]
        level.append([row[i] * row[i + 1] for i in range(0, len(row) - 1, 2)] + (row[-1:] if len(row) % 2 else []))
    inverse = [amplitude / (level[-1][0] * frequency)]
    for row in reversed(level[:-1]):
        finer = []
        for i in range(len(row)):
            partner = i ^ 1
            finer.append(inverse[i // 2] * row[partner] if partner < len(row) else inverse[i // 2])
        inverse = finer
    return [h * v for h, v in zip(gap, inverse)]


def chunk_kernel(groups, energies, first, last, parts, scale, *refs):
    shift_ref, own_ref, pair_ref = refs[:3]
    items = refs[3 : 3 + groups]
    rest = list(refs[3 + groups :])
    acc_in = None if first else rest.pop(0)
    if last:
        chosen_ref, out_ref, acc_ref, work_ref = rest
    else:
        acc_ref, work_ref = rest
    step = pl.program_id(0)
    bands = own_ref.shape[0]
    width = own_ref.shape[2]
    states = own_ref.shape[1]
    height = items[0].shape[1]
    columns = height * groups

    @pl.when(step == 0)
    def _():
        acc_ref[...] = jnp.zeros_like(acc_ref) if first else acc_in[...]

    shift = [shift_ref[i] for i in range(2 * bands * energies)]
    piece = min(width, 2 * LANES)

    def fill(t, carry):
        lanes = pl.ds(pl.multiple_of(t * piece, LANES), piece)
        for g, item in enumerate(items):
            for top in range(0, height, 16):
                tall = min(16, height - top)
                amplitude = item[0, top : top + tall, lanes].astype(jnp.float32)
                frequency = item[1, top : top + tall, lanes].astype(jnp.float32)
                blocks = screened_block(shift, amplitude, frequency)
                for i, block in enumerate(blocks):
                    m, e = divmod(i, energies)
                    at = e * columns + g * height + top
                    work_ref[m, at : at + tall, lanes] = block.astype(jnp.bfloat16)
        return carry

    lax.fori_loop(0, width // piece, fill, 0)
    for m in range(2 * bands):
        elements = own_ref[m] if m < bands else pair_ref[m - bands]
        acc_ref[m] += lax.dot_general(
            elements, work_ref[m], contract_minor, preferred_element_type=jnp.float32
        )

    if last:

        @pl.when(step == pl.num_programs(0) - 1)
        def _():
            rows = states // parts
            split = out_ref.shape[1] // (energies * rows)
            wide = states // split
            for e in range(energies):
                total = jnp.zeros((states, states), jnp.float32)
                for m in range(2 * bands):
                    block = acc_ref[m, :, e * columns : (e + 1) * columns]
                    upper = block.astype(jnp.bfloat16)
                    lower = (block - upper.astype(jnp.float32)).astype(jnp.bfloat16)
                    picked = chosen_ref[m]
                    total += jnp.dot(upper, picked, preferred_element_type=jnp.float32)
                    total += jnp.dot(lower, picked, preferred_element_type=jnp.float32)
                total = total * scale
                for p in range(parts):
                    for k in range(split):
                        at = (k * energies + e) * rows
                        out_ref[p, at : at + rows, :] = total[
                            p * rows : (p + 1) * rows, k * wide : (k + 1) * wide
                        ]


def chunk(index, count, shift, mel, pair, items, acc, chosen, parts, scale):
    bands, states, rows = mel.shape
    size = rows // count
    width = largest_block(size, 1024)
    steps = size // width
    base = index * steps
    groups = len(items)
    height = items[0].shape[1]
    columns = groups * height
    energies = shift.shape[0] // (2 * bands)
    first, last = acc is None, chosen is not None
    acc_shape = (2 * bands, states, energies * columns)
    acc_spec = pl.BlockSpec(acc_shape, lambda i: (0, 0, 0))
    mel_spec = pl.BlockSpec((bands, states, width), lambda i: (0, 0, base + i))
    operands = [shift, mel, pair, *items]
    in_specs = [pl.BlockSpec(memory_space=pltpu.SMEM), mel_spec, mel_spec]
    in_specs += [pl.BlockSpec((2, height, width), lambda i: (0, 0, i))] * groups
    if not first:
        operands.append(acc)
        in_specs.append(acc_spec)
    scratch = [VM((2 * bands, energies * columns, width), jnp.bfloat16)]
    alias = {}
    if last:
        operands.append(chosen)
        in_specs.append(pl.BlockSpec(chosen.shape, lambda i: (0, 0, 0)))
        split = max(1, states // LANES)
        out_shape = jax.ShapeDtypeStruct(
            (parts, split * energies * (states // parts), states // split), jnp.float32
        )
        out_spec = pl.BlockSpec(out_shape.shape, lambda i: (0, 0, 0))
        scratch = [VM(acc_shape, jnp.float32)] + scratch
    else:
        out_shape = jax.ShapeDtypeStruct(acc_shape, jnp.float32)
        out_spec = acc_spec
        if not first:
            alias = {len(operands) - 1: 0}
    flops = 2 * 2 * bands * energies * states * columns * size
    return pl.pallas_call(
        functools.partial(chunk_kernel, groups, energies, first, last, parts, scale),
        grid=(steps,),
        in_specs=in_specs,
        out_specs=out_spec,
        out_shape=out_shape,
        scratch_shapes=scratch,
        input_output_aliases=alias,
        cost_estimate=pl.CostEstimate(
            flops=4 * flops, bytes_accessed=8 * bands * states * size, transcendentals=0
        ),
        name="chunk",
    )(*operands)


def spread_kernel(count, chip_ref, a_ref, b_ref, *out_refs):
    tall = out_refs[0].shape[0]
    for d in range(count):
        at = pl.ds((chip_ref[0] ^ d) * tall, tall)
        out_refs[d][...] = a_ref[at, :] + b_ref[at, :]


def spread(chip, count, a, b):
    rows, width = a.shape
    tall = rows // count
    if tall % 8:
        both = a + b
        return [
            lax.dynamic_slice_in_dim(both, (chip ^ d) * tall, tall, 0) for d in range(count)
        ]
    return pl.pallas_call(
        functools.partial(spread_kernel, count),
        in_specs=[pl.BlockSpec(memory_space=pltpu.SMEM)] + [pl.BlockSpec(memory_space=VM)] * 2,
        out_specs=[pl.BlockSpec(memory_space=VM)] * count,
        out_shape=[jax.ShapeDtypeStruct((tall, width), jnp.float32)] * count,
        name="spread",
    )(chip.reshape(1), a, b)


def settle_kernel(count, energies, place_ref, *refs):
    pieces, out_ref = refs[:count], refs[count]
    tall, wide = pieces[0].shape
    rows = out_ref.shape[1]
    per_energy = rows // tall
    for d in range(count):
        at = place_ref[d]
        lanes = at // (energies * per_energy)
        e = (at // per_energy) % energies
        top = (at % per_energy) * tall
        out_ref[e, pl.ds(top, tall), pl.ds(pl.multiple_of(lanes * wide, wide), wide)] = pieces[d][...]


def settle(place, pieces, energies, rows, states):
    tall, wide = pieces[0].shape
    if tall % 8:
        slot = jnp.zeros_like(place).at[place].set(jnp.arange(len(pieces), dtype=jnp.int32))
        whole = jnp.stack(pieces)[slot].reshape(states // wide, energies, rows, wide)
        return whole.transpose(1, 2, 0, 3).reshape(energies, rows, states)
    return pl.pallas_call(
        functools.partial(settle_kernel, len(pieces), energies),
        in_specs=[pl.BlockSpec(memory_space=pltpu.SMEM)]
        + [pl.BlockSpec(memory_space=VM)] * len(pieces),
        out_specs=pl.BlockSpec(memory_space=VM),
        out_shape=jax.ShapeDtypeStruct((energies, rows, states), jnp.float32),
        name="settle",
    )(place, *pieces)


def local(bands_total, pw_total, chunks, mel, pole_amp, pole_freq, band_energy, occupation, column_map, energies):
    bands, states, rows = mel.shape
    columns = pole_amp.shape[1]
    chips = bands_total // 2
    band_at = lax.axis_index("band")
    pw_at = lax.axis_index("pw")
    core, chip = band_at % 2, band_at // 2
    energy_count = energies.shape[0]

    pair = swap(mel, "band", bands_total, 1)
    sign = (2 * occupation - 1).astype(jnp.float32)
    shift = sign[:, None] * (energies[None, :] - band_energy[:, None])
    shift = jnp.concatenate([shift, swap(shift, "band", bands_total, 1)]).reshape(-1)

    count = min(chunks, rows // LANES)
    size = rows // count
    amp_t, freq_t = pole_amp.T, pole_freq.T
    slots = []
    for c in range(count):
        window = slice(c * size, (c + 1) * size)
        slots.append({0: jnp.stack([amp_t[:, window], freq_t[:, window]])})
    tops = [1 << b for b in reversed(range(chips.bit_length() - 1))]
    for c in range(count):
        have = slots[c]
        for top in tops:
            for s in list(have):
                have[s | top] = swap(have[s], "band", bands_total, 2 * top)

    order = jnp.arange(chips, dtype=jnp.int32) ^ chip
    by_device = column_map.reshape(bands_total, columns)
    mine = by_device[2 * order + core].reshape(-1)
    theirs = by_device[2 * order + (1 - core)].reshape(-1)
    index = jnp.concatenate([mine, theirs]) - pw_at * rows
    picked = pick(mel, index, sign)
    for b in range(pw_total.bit_length() - 1):
        picked = picked + swap(picked, "pw", pw_total, 1 << b)
    half = picked.shape[1] // 2
    chosen = jnp.concatenate([picked[:, :half], swap(picked[:, half:], "band", bands_total, 1)])

    scale = 1.0 / math.sqrt(rows * pw_total * column_map.shape[0] * bands * bands_total)
    acc = None
    for c in range(count):
        items = [slots[c][s] for s in range(chips)]
        if columns % 16:
            items = [jnp.concatenate(items, axis=1)]
        final = chosen if c == count - 1 else None
        acc = chunk(c, count, shift, mel, pair, items, acc, final, pw_total, scale)
    partial = acc

    tall = partial.shape[1] // 2

    def half_of(x, which):
        return lax.dynamic_slice_in_dim(x, which * tall, tall, 1)

    partial = half_of(partial, core) + swap(half_of(partial, 1 - core), "band", bands_total, 1)
    parts = pw_total
    while parts > 2:
        parts //= 2
        bit = (pw_at // parts) % 2
        keep = lax.dynamic_slice_in_dim(partial, bit * parts, parts, 0)
        give = lax.dynamic_slice_in_dim(partial, (1 - bit) * parts, parts, 0)
        partial = keep + swap(give, "pw", pw_total, parts)
    if parts == 2:
        bit = pw_at % 2
        keep = lax.dynamic_index_in_dim(partial, bit, 0, False)
        got = swap(lax.dynamic_index_in_dim(partial, 1 - bit, 0, False), "pw", pw_total, 1)
    else:
        keep = partial[0]
        got = jnp.zeros_like(keep)
    pieces = spread(chip, chips, keep, got)
    total = pieces[0]
    for d in range(1, chips):
        total = total + swap(pieces[d], "band", bands_total, 2 * d)
    final = [total] + [swap(total, "band", bands_total, d) for d in range(1, bands_total)]
    source = jnp.arange(bands_total, dtype=jnp.int32) ^ band_at
    place = (source % 2) * chips + source // 2
    return settle(place, final, energy_count, states // pw_total, states)


def solution(mesh):
    bands_total, pw_total = mesh.shape["band"], mesh.shape["pw"]
    return jax.shard_map(
        functools.partial(local, bands_total, pw_total, 8),
        mesh=mesh,
        in_specs=(
            P("band", None, "pw"),
            P("pw", "band"),
            P("pw", "band"),
            P("band"),
            P("band"),
            P(),
            P(),
        ),
        out_specs=P(None, "pw", None),
        check_vma=False,
    )
```

```python
import functools
import math

import jax
import jax.numpy as jnp
from jax import lax
from jax.experimental import pallas as pl
from jax.experimental.pallas import tpu as pltpu
from jax.sharding import PartitionSpec as P


broadening = 0.4
LANES = 128
VM = pltpu.VMEM


CHUNKS = 4

contract_minor = (((1,), (1,)), ((), ()))


def swap(value, axis, size, mask):
    return lax.ppermute(value, axis, [(i, i ^ mask) for i in range(size)])


def largest_block(extent, limit):
    block = extent
    while block > limit and block % (2 * LANES) == 0:
        block //= 2
    return block


def pick_kernel(sign_ref, index_ref, mel_ref, out_ref, acc_ref):
    step = pl.program_id(0)
    bands, _, width = mel_ref.shape
    columns = index_ref.shape[0]
    lane = lax.broadcasted_iota(jnp.int32, (columns, width), 1) + step * width
    hot = (lane == index_ref[...]).astype(jnp.float32).astype(jnp.bfloat16)

    @pl.when(step == 0)
    def _():
        acc_ref[...] = jnp.zeros_like(acc_ref)

    for m in range(bands):
        acc_ref[m] += lax.dot_general(
            hot, mel_ref[m], contract_minor, preferred_element_type=jnp.float32
        )

    @pl.when(step == pl.num_programs(0) - 1)
    def _():
        for m in range(bands):
            out_ref[m] = (acc_ref[m] * sign_ref[m]).astype(out_ref.dtype)


def pick(mel, index, sign):
    bands, states, rows = mel.shape
    columns = index.shape[0]
    width = largest_block(rows, 1024)
    return pl.pallas_call(
        pick_kernel,
        grid=(rows // width,),
        in_specs=[
            pl.BlockSpec(memory_space=pltpu.SMEM),
            pl.BlockSpec((columns, 1), lambda i: (0, 0)),
            pl.BlockSpec((bands, states, width), lambda i: (0, 0, i)),
        ],
        out_specs=pl.BlockSpec((bands, columns, states), lambda i: (0, 0, 0)),
        out_shape=jax.ShapeDtypeStruct((bands, columns, states), jnp.bfloat16),
        scratch_shapes=[VM((bands, columns, states), jnp.float32)],
        cost_estimate=pl.CostEstimate(
            flops=2 * bands * columns * states * rows,
            bytes_accessed=2 * mel.size,
            transcendentals=0,
        ),
        name="pick",
    )(sign, index.reshape(columns, 1), mel)


def screened_block(shift, amplitude, frequency):
    gap = [frequency + s for s in shift]
    level = [[h * h + broadening * broadening for h in gap]]
    while len(level[-1]) > 1:
        row = level[-1]
        level.append([row[i] * row[i + 1] for i in range(0, len(row) - 1, 2)] + (row[-1:] if len(row) % 2 else []))
    inverse = [amplitude / (level[-1][0] * frequency)]
    for row in reversed(level[:-1]):
        finer = []
        for i in range(len(row)):
            partner = i ^ 1
            finer.append(inverse[i // 2] * row[partner] if partner < len(row) else inverse[i // 2])
        inverse = finer
    return [h * v for h, v in zip(gap, inverse)]


def chunk_kernel(groups, energies, first, last, parts, scale, *refs):
    shift_ref, own_ref, pair_ref = refs[:3]
    items = refs[3 : 3 + groups]
    rest = list(refs[3 + groups :])
    acc_in = None if first else rest.pop(0)
    if last:
        chosen_ref, out_ref, acc_ref, work_ref = rest
    else:
        acc_ref, work_ref = rest
    step = pl.program_id(0)
    bands = own_ref.shape[0]
    width = own_ref.shape[2]
    states = own_ref.shape[1]
    height = items[0].shape[1]
    columns = height * groups

    @pl.when(step == 0)
    def _():
        acc_ref[...] = jnp.zeros_like(acc_ref) if first else acc_in[...]

    shift = [shift_ref[i] for i in range(2 * bands * energies)]
    piece = min(width, 2 * LANES)

    def fill(t, carry):
        lanes = pl.ds(pl.multiple_of(t * piece, LANES), piece)
        for g, item in enumerate(items):
            for top in range(0, height, 16):
                tall = min(16, height - top)
                amplitude = item[0, top : top + tall, lanes].astype(jnp.float32)
                frequency = item[1, top : top + tall, lanes].astype(jnp.float32)
                blocks = screened_block(shift, amplitude, frequency)
                for i, block in enumerate(blocks):
                    m, e = divmod(i, energies)
                    at = e * columns + g * height + top
                    work_ref[m, at : at + tall, lanes] = block.astype(jnp.bfloat16)
        return carry

    lax.fori_loop(0, width // piece, fill, 0)
    for m in range(2 * bands):
        elements = own_ref[m] if m < bands else pair_ref[m - bands]
        acc_ref[m] += lax.dot_general(
            elements, work_ref[m], contract_minor, preferred_element_type=jnp.float32
        )

    if last:

        @pl.when(step == pl.num_programs(0) - 1)
        def _():
            rows = states // parts
            wide = states // 2
            for e in range(energies):
                total = jnp.zeros((states, states), jnp.float32)
                for m in range(2 * bands):
                    block = acc_ref[m, :, e * columns : (e + 1) * columns]
                    upper = block.astype(jnp.bfloat16)
                    lower = (block - upper.astype(jnp.float32)).astype(jnp.bfloat16)
                    picked = chosen_ref[m]
                    total += jnp.dot(upper, picked, preferred_element_type=jnp.float32)
                    total += jnp.dot(lower, picked, preferred_element_type=jnp.float32)
                total = total * scale
                for p in range(parts):
                    for k in range(2):
                        out_ref[k, p, e * rows : (e + 1) * rows, :] = total[
                            p * rows : (p + 1) * rows, k * wide : (k + 1) * wide
                        ]


def chunk(index, count, shift, mel, pair, items, acc, chosen, parts, scale):
    bands, states, rows = mel.shape
    size = rows // count
    width = largest_block(size, 1024)
    steps = size // width
    base = index * steps
    groups = len(items)
    height = items[0].shape[1]
    columns = groups * height
    energies = shift.shape[0] // (2 * bands)
    first, last = acc is None, chosen is not None
    acc_shape = (2 * bands, states, energies * columns)
    acc_spec = pl.BlockSpec(acc_shape, lambda i: (0, 0, 0))
    mel_spec = pl.BlockSpec((bands, states, width), lambda i: (0, 0, base + i))
    operands = [shift, mel, pair, *items]
    in_specs = [pl.BlockSpec(memory_space=pltpu.SMEM), mel_spec, mel_spec]
    in_specs += [pl.BlockSpec((2, height, width), lambda i: (0, 0, i))] * groups
    if not first:
        operands.append(acc)
        in_specs.append(acc_spec)
    scratch = [VM((2 * bands, energies * columns, width), jnp.bfloat16)]
    alias = {}
    if last:
        operands.append(chosen)
        in_specs.append(pl.BlockSpec(chosen.shape, lambda i: (0, 0, 0)))
        out_shape = jax.ShapeDtypeStruct(
            (2, parts, energies * (states // parts), states // 2), jnp.float32
        )
        out_spec = pl.BlockSpec(out_shape.shape, lambda i: (0, 0, 0, 0))
        scratch = [VM(acc_shape, jnp.float32)] + scratch
    else:
        out_shape = jax.ShapeDtypeStruct(acc_shape, jnp.float32)
        out_spec = acc_spec
        if not first:
            alias = {len(operands) - 1: 0}
    flops = 2 * 2 * bands * energies * states * columns * size
    return pl.pallas_call(
        functools.partial(chunk_kernel, groups, energies, first, last, parts, scale),
        grid=(steps,),
        in_specs=in_specs,
        out_specs=out_spec,
        out_shape=out_shape,
        scratch_shapes=scratch,
        input_output_aliases=alias,
        cost_estimate=pl.CostEstimate(
            flops=4 * flops, bytes_accessed=8 * bands * states * size, transcendentals=0
        ),
        name="chunk",
    )(*operands)


def spread_kernel(count, chip_ref, a_ref, b_ref, *out_refs):
    tall = out_refs[0].shape[0]
    for d in range(count):
        at = pl.ds((chip_ref[0] ^ d) * tall, tall)
        out_refs[d][...] = a_ref[at, :] + b_ref[at, :]


def spread(chip, count, a, b):
    rows, width = a.shape
    tall = rows // count
    if tall % 8:
        both = a + b
        return [
            lax.dynamic_slice_in_dim(both, (chip ^ d) * tall, tall, 0) for d in range(count)
        ]
    return pl.pallas_call(
        functools.partial(spread_kernel, count),
        in_specs=[pl.BlockSpec(memory_space=pltpu.SMEM)] + [pl.BlockSpec(memory_space=VM)] * 2,
        out_specs=[pl.BlockSpec(memory_space=VM)] * count,
        out_shape=[jax.ShapeDtypeStruct((tall, width), jnp.float32)] * count,
        name="spread",
    )(chip.reshape(1), a, b)


def settle_kernel(count, place_ref, *refs):
    pieces, out_ref = refs[:count], refs[count]
    _, tall, wide = pieces[0].shape
    per_energy = out_ref.shape[1] // tall
    core, chip = place_ref[0], place_ref[1]
    for d in range(count):
        at = chip ^ d
        e, top = at // per_energy, (at % per_energy) * tall
        for r in range(2):
            lanes = pl.ds(pl.multiple_of((core ^ r) * wide, wide), wide)
            out_ref[e, pl.ds(pl.multiple_of(top, tall), tall), lanes] = pieces[d][r]


def settle(core, chip, pieces, energies, rows, states):
    _, tall, _ = pieces[0].shape
    count = len(pieces)
    if tall % 8:
        order = jnp.arange(count, dtype=jnp.int32) ^ chip
        cores = jnp.arange(2, dtype=jnp.int32) ^ core
        whole = jnp.stack(pieces)[order][:, cores].transpose(0, 2, 1, 3)
        return whole.reshape(energies, rows, states)
    place = jnp.stack([core, chip]).astype(jnp.int32)
    return pl.pallas_call(
        functools.partial(settle_kernel, count),
        in_specs=[pl.BlockSpec(memory_space=pltpu.SMEM)]
        + [pl.BlockSpec(memory_space=VM)] * count,
        out_specs=pl.BlockSpec(memory_space=VM),
        out_shape=jax.ShapeDtypeStruct((energies, rows, states), jnp.float32),
        name="settle",
    )(place, *pieces)


def local(bands_total, pw_total, chunks, mel, pole_amp, pole_freq, band_energy, occupation, column_map, energies):
    bands, states, rows = mel.shape
    columns = pole_amp.shape[1]
    chips = bands_total // 2
    band_at = lax.axis_index("band")
    pw_at = lax.axis_index("pw")
    core, chip = band_at % 2, band_at // 2
    energy_count = energies.shape[0]

    pair = swap(mel, "band", bands_total, 1)
    sign = (2 * occupation - 1).astype(jnp.float32)
    shift = sign[:, None] * (energies[None, :] - band_energy[:, None])
    shift = jnp.concatenate([shift, swap(shift, "band", bands_total, 1)]).reshape(-1)

    count = min(chunks, rows // LANES)
    size = rows // count
    amp_t, freq_t = pole_amp.T, pole_freq.T
    slots = []
    for c in range(count):
        window = slice(c * size, (c + 1) * size)
        slots.append({0: jnp.stack([amp_t[:, window], freq_t[:, window]])})
    tops = [1 << b for b in reversed(range(chips.bit_length() - 1))]
    for c in range(count):
        have = slots[c]
        for top in tops:
            for s in list(have):
                if c == count - 1 and s == tops[0] and top == 1:
                    continue
                have[s | top] = swap(have[s], "band", bands_total, 2 * top)
        if tops[0] | 1 not in have:
            have[tops[0] | 1] = swap(have[1], "band", bands_total, 2 * tops[0])

    order = jnp.arange(chips, dtype=jnp.int32) ^ chip
    by_device = column_map.reshape(bands_total, columns)
    mine = by_device[2 * order + core].reshape(-1)
    theirs = by_device[2 * order + (1 - core)].reshape(-1)
    index = jnp.concatenate([mine, theirs]) - pw_at * rows
    picked = pick(mel, index, sign)
    for b in range(pw_total.bit_length() - 1):
        picked = picked + swap(picked, "pw", pw_total, 1 << b)
    half = picked.shape[1] // 2
    chosen = jnp.concatenate([picked[:, :half], swap(picked[:, half:], "band", bands_total, 1)])

    scale = 1.0 / math.sqrt(rows * pw_total * column_map.shape[0] * bands * bands_total)
    acc = None
    for c in range(count):
        items = [slots[c][s] for s in range(chips)]
        if columns % 16:
            items = [jnp.concatenate(items, axis=1)]
        final = chosen if c == count - 1 else None
        acc = chunk(c, count, shift, mel, pair, items, acc, final, pw_total, scale)
    partial = acc

    keep = lax.dynamic_index_in_dim(partial, core, 0, False)
    partial = keep + swap(
        lax.dynamic_index_in_dim(partial, 1 - core, 0, False), "band", bands_total, 1
    )
    parts = pw_total
    while parts > 2:
        parts //= 2
        bit = (pw_at // parts) % 2
        keep = lax.dynamic_slice_in_dim(partial, bit * parts, parts, 0)
        give = lax.dynamic_slice_in_dim(partial, (1 - bit) * parts, parts, 0)
        partial = keep + swap(give, "pw", pw_total, parts)
    if parts == 2:
        bit = pw_at % 2
        keep = lax.dynamic_index_in_dim(partial, bit, 0, False)
        got = swap(lax.dynamic_index_in_dim(partial, 1 - bit, 0, False), "pw", pw_total, 1)
    else:
        keep = partial[0]
        got = jnp.zeros_like(keep)
    pieces = spread(chip, chips, keep, got)
    total = pieces[0]
    for d in range(1, chips):
        total = total + swap(pieces[d], "band", bands_total, 2 * d)
    both = jnp.stack([total, swap(total, "band", bands_total, 1)])
    final = [both] + [swap(both, "band", bands_total, 2 * d) for d in range(1, chips)]
    return settle(core, chip, final, energy_count, states // pw_total, states)


def solution(mesh):
    bands_total, pw_total = mesh.shape["band"], mesh.shape["pw"]

    def body(*args):
        return local(bands_total, pw_total, CHUNKS, *args)

    return jax.shard_map(
        body,
        mesh=mesh,
        in_specs=(
            P("band", None, "pw"),
            P("pw", "band"),
            P("pw", "band"),
            P("band"),
            P("band"),
            P(),
            P(),
        ),
        out_specs=P(None, "pw", None),
        check_vma=False,
    )
```

```python
import functools
import math

import jax
import jax.numpy as jnp
from jax import lax
from jax.experimental import pallas as pl
from jax.experimental.pallas import tpu as pltpu
from jax.sharding import PartitionSpec as P


broadening = 0.4
LANES = 128
VM = pltpu.VMEM


CHUNKS = 4

contract_minor = (((1,), (1,)), ((), ()))


def swap(value, axis, size, mask):
    return lax.ppermute(value, axis, [(i, i ^ mask) for i in range(size)])


def largest_block(extent, limit):
    block = extent
    while block > limit and block % (2 * LANES) == 0:
        block //= 2
    return block


def pick_kernel(height, place_ref, occupation_ref, map_ref, mel_ref, mine_ref, theirs_ref, index_ref, acc_ref):
    step = pl.program_id(0)
    bands, _, width = mel_ref.shape
    columns = map_ref.shape[0]
    chips = columns // (2 * height)

    @pl.when(step == 0)
    def _():
        acc_ref[...] = jnp.zeros_like(acc_ref)
        for other in range(2):
            for d in range(chips):
                device = 2 * (place_ref[1] ^ d) + (place_ref[0] ^ other)
                at = (other * chips + d) * height
                source = pl.ds(pl.multiple_of(device * height, height), height)
                index_ref[at : at + height, :] = map_ref[source, :] - place_ref[2]

    piece = min(width, 2 * LANES)
    index = index_ref[...] - step * width
    lane = lax.broadcasted_iota(jnp.int32, (columns, piece), 1)
    for low in range(0, width, piece):
        hot = (lane == index - low).astype(jnp.float32).astype(jnp.bfloat16)
        for m in range(bands):
            acc_ref[m] += lax.dot_general(
                hot,
                mel_ref[m, :, low : low + piece],
                contract_minor,
                preferred_element_type=jnp.float32,
            )

    @pl.when(step == pl.num_programs(0) - 1)
    def _():
        half = columns // 2
        for m in range(bands):
            sign = (2 * occupation_ref[m] - 1).astype(jnp.float32)
            signed = (acc_ref[m] * sign).astype(jnp.bfloat16)
            mine_ref[m] = signed[:half]
            theirs_ref[m] = signed[half:]


def pick(place, occupation, column_map, mel, devices):
    bands, states, rows = mel.shape
    columns = column_map.shape[0]
    width = largest_block(rows, 1024)
    out = jax.ShapeDtypeStruct((bands, columns // 2, states), jnp.bfloat16)
    out_spec = pl.BlockSpec(out.shape, lambda i: (0, 0, 0))
    height = columns // devices
    column_map = column_map.reshape(columns, 1)
    if height % 8:
        slot = jnp.arange(devices, dtype=jnp.int32)
        device = 2 * ((slot % (devices // 2)) ^ place[1]) + (slot // (devices // 2) ^ place[0])
        column_map = column_map.reshape(devices, height)[device].reshape(columns, 1)
        place = jnp.stack([jnp.zeros_like(place[0]), jnp.zeros_like(place[0]), place[2]])
        height = columns // 2
    return pl.pallas_call(
        functools.partial(pick_kernel, height),
        grid=(rows // width,),
        in_specs=[
            pl.BlockSpec(memory_space=pltpu.SMEM),
            pl.BlockSpec(memory_space=pltpu.SMEM),
            pl.BlockSpec((columns, 1), lambda i: (0, 0)),
            pl.BlockSpec((bands, states, width), lambda i: (0, 0, i)),
        ],
        out_specs=[out_spec, out_spec],
        out_shape=[out, out],
        scratch_shapes=[VM((columns, 1), jnp.int32), VM((bands, columns, states), jnp.float32)],
        cost_estimate=pl.CostEstimate(
            flops=2 * bands * columns * states * rows,
            bytes_accessed=2 * mel.size,
            transcendentals=0,
        ),
        name="pick",
    )(place, occupation, column_map, mel)


def screened_block(shift, amplitude, frequency):
    gap = [frequency + s for s in shift]
    level = [[h * h + broadening * broadening for h in gap]]
    while len(level[-1]) > 1:
        row = level[-1]
        level.append([row[i] * row[i + 1] for i in range(0, len(row) - 1, 2)] + (row[-1:] if len(row) % 2 else []))
    inverse = [amplitude / (level[-1][0] * frequency)]
    for row in reversed(level[:-1]):
        finer = []
        for i in range(len(row)):
            partner = i ^ 1
            finer.append(inverse[i // 2] * row[partner] if partner < len(row) else inverse[i // 2])
        inverse = finer
    return [h * v for h, v in zip(gap, inverse)]


def chunk_kernel(groups, energies, first, last, parts, scale, *refs):
    own_shift, pair_shift, own_ref, pair_ref = refs[:4]
    items = refs[4 : 4 + groups]
    rest = list(refs[4 + groups :])
    acc_in = None if first else rest.pop(0)
    work_ref = rest.pop()
    if last:
        acc_ref = rest.pop()
        give_ref, keep_ref = rest.pop(), rest.pop()
        place_ref, *chosen = rest
    else:
        (acc_ref,) = rest
    step = pl.program_id(0)
    bands, states, width = own_ref.shape
    height = items[0].shape[1]
    columns = height * groups

    @pl.when(step == 0)
    def _():
        acc_ref[...] = jnp.zeros_like(acc_ref) if first else acc_in[...]

    shift = [ref[m, e] for ref in (own_shift, pair_shift) for m in range(bands) for e in range(energies)]
    piece = min(width, 2 * LANES)
    span = min(width, 4 * LANES)
    for low in range(0, width, span):
        for left in range(low, low + span, piece):
            lanes = slice(left, left + piece)
            for g, item in enumerate(items):
                for top in range(0, height, 16):
                    tall = min(16, height - top)
                    amplitude = item[0, top : top + tall, lanes].astype(jnp.float32)
                    frequency = item[1, top : top + tall, lanes].astype(jnp.float32)
                    blocks = screened_block(shift, amplitude, frequency)
                    for i, block in enumerate(blocks):
                        m, e = divmod(i, energies)
                        at = e * columns + g * height + top
                        work_ref[m, at : at + tall, lanes] = block.astype(jnp.bfloat16)
        for m in range(2 * bands):
            elements = own_ref if m < bands else pair_ref
            acc_ref[m] += lax.dot_general(
                elements[m % bands, :, low : low + span],
                work_ref[m, :, low : low + span],
                contract_minor,
                preferred_element_type=jnp.float32,
            )

    if last:

        @pl.when(step == pl.num_programs(0) - 1)
        def _():
            rows = states // parts
            wide = states // 2
            half = len(chosen) // 2
            picked = []
            for m in range(2 * bands):
                group = chosen[:half] if m < bands else chosen[half:]
                value = group[0][m % bands]
                for more in group[1:]:
                    value = value + more[m % bands]
                picked.append(value)
            for e in range(energies):
                total = jnp.zeros((states, states), jnp.float32)
                for m in range(2 * bands):
                    block = acc_ref[m, :, e * columns : (e + 1) * columns]
                    upper = block.astype(jnp.bfloat16)
                    lower = (block - upper.astype(jnp.float32)).astype(jnp.bfloat16)
                    total += jnp.dot(upper, picked[m], preferred_element_type=jnp.float32)
                    total += jnp.dot(lower, picked[m], preferred_element_type=jnp.float32)
                total = total * scale
                for core in range(2):

                    @pl.when(place_ref[0] == core)
                    def _():
                        for p in range(parts):
                            block = total[p * rows : (p + 1) * rows]
                            at = slice(e * rows, (e + 1) * rows)
                            other = 1 - core
                            keep_ref[p, at, :] = block[:, core * wide : (core + 1) * wide]
                            give_ref[p, at, :] = block[:, other * wide : (other + 1) * wide]


def chunk(index, count, shifts, mel, pair, items, acc, place, chosen, parts, scale):
    bands, states, rows = mel.shape
    size = rows // count
    width = largest_block(size, 1024)
    steps = size // width
    base = index * steps
    groups = len(items)
    height = items[0].shape[1]
    columns = groups * height
    energies = shifts[0].shape[1]
    first, last = acc is None, chosen is not None
    acc_shape = (2 * bands, states, energies * columns)
    acc_spec = pl.BlockSpec(acc_shape, lambda i: (0, 0, 0))
    mel_spec = pl.BlockSpec((bands, states, width), lambda i: (0, 0, base + i))
    smem = pl.BlockSpec(memory_space=pltpu.SMEM)
    operands = [*shifts, mel, pair, *items]
    in_specs = [smem, smem, mel_spec, mel_spec]
    in_specs += [pl.BlockSpec((2, height, width), lambda i: (0, 0, i))] * groups
    if not first:
        operands.append(acc)
        in_specs.append(acc_spec)
    scratch = [VM((2 * bands, energies * columns, width), jnp.bfloat16)]
    alias = {}
    if last:
        operands += [place, *chosen]
        in_specs += [smem] + [pl.BlockSpec(c.shape, lambda i: (0, 0, 0)) for c in chosen]
        half = jax.ShapeDtypeStruct((parts, energies * (states // parts), states // 2), jnp.float32)
        out_shape = [half, half]
        out_spec = [pl.BlockSpec(half.shape, lambda i: (0, 0, 0))] * 2
        scratch = [VM(acc_shape, jnp.float32)] + scratch
    else:
        out_shape = jax.ShapeDtypeStruct(acc_shape, jnp.float32)
        out_spec = acc_spec
        if not first:
            alias = {len(operands) - 1: 0}
    flops = 2 * 2 * bands * energies * states * columns * size
    return pl.pallas_call(
        functools.partial(chunk_kernel, groups, energies, first, last, parts, scale),
        grid=(steps,),
        in_specs=in_specs,
        out_specs=out_spec,
        out_shape=out_shape,
        scratch_shapes=scratch,
        input_output_aliases=alias,
        cost_estimate=pl.CostEstimate(
            flops=4 * flops, bytes_accessed=8 * bands * states * size, transcendentals=0
        ),
        name="chunk",
    )(*operands)


def part_kernel(which, count, place_ref, a_ref, b_ref, *out_refs):
    tall = out_refs[0].shape[0]
    for d in range(count):
        if len(a_ref.shape) == 3:
            own = place_ref[which] ^ d
            out_refs[d][...] = a_ref[own] + b_ref[own]
        else:
            at = pl.ds(pl.multiple_of((place_ref[which] ^ d) * tall, tall), tall)
            out_refs[d][...] = a_ref[at, :] + b_ref[at, :]


def part(place, which, count, a, b):
    shape = a.shape[1:] if a.ndim == 3 else (a.shape[0] // count, a.shape[1])
    if shape[0] % 8:
        both = (a + b).reshape((count,) + shape)
        return [lax.dynamic_index_in_dim(both, place[which] ^ d, 0, False) for d in range(count)]
    whole = [pl.BlockSpec(x.shape, lambda n=x.ndim: (0,) * n) for x in (a, b)]
    return pl.pallas_call(
        functools.partial(part_kernel, which, count),
        in_specs=[pl.BlockSpec(memory_space=pltpu.SMEM)] + whole,
        out_specs=[pl.BlockSpec(shape, lambda: (0, 0))] * count,
        out_shape=[jax.ShapeDtypeStruct(shape, jnp.float32)] * count,
        name="part",
    )(place, a, b)


def settle_kernel(place_ref, *refs):
    pieces, out_ref = refs[:-1], refs[-1]
    near, _, tall, wide = pieces[0].shape
    per_energy = out_ref.shape[1] // tall
    for d, piece in enumerate(pieces):
        for n in range(near):
            at = (place_ref[3] ^ n) * len(pieces) + (place_ref[4] ^ d)
            e, top = at // per_energy, (at % per_energy) * tall
            for r in range(2):
                lanes = pl.ds(pl.multiple_of((place_ref[0] ^ r) * wide, wide), wide)
                out_ref[e, pl.ds(pl.multiple_of(top, tall), tall), lanes] = piece[n, r]


def settle(place, pieces, energies, rows, states):
    near, _, tall, _ = pieces[0].shape
    far = len(pieces)
    shape = (energies, rows, states)
    if tall % 8:
        order = [jnp.arange(n, dtype=jnp.int32) ^ place[i] for n, i in ((far, 4), (near, 3), (2, 0))]
        whole = jnp.stack(pieces)[order[0]][:, order[1]][:, :, order[2]]
        return whole.transpose(1, 0, 3, 2, 4).reshape(shape)
    return pl.pallas_call(
        settle_kernel,
        in_specs=[pl.BlockSpec(memory_space=pltpu.SMEM)]
        + [pl.BlockSpec(pieces[0].shape, lambda: (0, 0, 0, 0))] * far,
        out_specs=pl.BlockSpec(shape, lambda: (0, 0, 0)),
        out_shape=jax.ShapeDtypeStruct(shape, jnp.float32),
        name="settle",
    )(place, *pieces)


def local(bands_total, pw_total, chunks, mel, pole_amp, pole_freq, band_energy, occupation, column_map, energies):
    bands, states, rows = mel.shape
    columns = pole_amp.shape[1]
    chips = bands_total // 2
    band_at = lax.axis_index("band")
    pw_at = lax.axis_index("pw")
    core, chip = band_at % 2, band_at // 2
    place = jnp.stack([core, chip, pw_at * rows, chip % 2, chip // 2, pw_at % 2]).astype(jnp.int32)
    energy_count = energies.shape[0]

    pair = swap(mel, "band", bands_total, 1)
    sign = (2 * occupation - 1).astype(jnp.float32)
    shift = sign[:, None] * (energies[None, :] - band_energy[:, None])
    shifts = (shift, swap(shift, "band", bands_total, 1))

    count = min(chunks, rows // LANES)
    size = rows // count
    amp_t, freq_t = pole_amp.T, pole_freq.T
    slots = []
    for c in range(count):
        window = slice(c * size, (c + 1) * size)
        slots.append({0: jnp.stack([amp_t[:, window], freq_t[:, window]])})
    tops = [1 << b for b in reversed(range(chips.bit_length() - 1))]
    for c in range(count):
        have = slots[c]
        for top in tops:
            for s in list(have):
                if c == count - 1 and s == tops[0] and top == 1:
                    continue
                have[s | top] = swap(have[s], "band", bands_total, 2 * top)
        if tops[0] | 1 not in have:
            have[tops[0] | 1] = swap(have[1], "band", bands_total, 2 * tops[0])

    mine, theirs = pick(place, occupation, column_map, mel, bands_total)
    chosen = []
    for value in (mine, swap(theirs, "band", bands_total, 1)):
        steps = pw_total.bit_length() - 1
        for b in range(steps - 1):
            value = value + swap(value, "pw", pw_total, 1 << b)
        chosen.append(value)
        if steps:
            chosen.append(swap(value, "pw", pw_total, 1 << (steps - 1)))

    scale = 1.0 / math.sqrt(rows * pw_total * column_map.shape[0] * bands * bands_total)
    acc = None
    for c in range(count):
        items = [slots[c][s] for s in range(chips)]
        if columns % 16:
            items = [jnp.concatenate(items, axis=1)]
        final = chosen if c == count - 1 else None
        acc = chunk(c, count, shifts, mel, pair, items, acc, place, final, pw_total, scale)
    keep, give = acc

    got = swap(give, "band", bands_total, 1)
    parts = pw_total
    while parts > 2 or parts == 1:
        keep, got = keep + got, jnp.zeros_like(keep)
        if parts == 1:
            break
        parts //= 2
        bit = (pw_at // parts) % 2
        send = lax.dynamic_slice_in_dim(keep, (1 - bit) * parts, parts, 0)
        keep = lax.dynamic_slice_in_dim(keep, bit * parts, parts, 0)
        got = swap(send, "pw", pw_total, parts)
    if parts == 2:
        keep, give = part(place, 5, 2, keep, got)
        got = swap(give, "pw", pw_total, 1)
    else:
        keep, got = keep[0], got[0]
    keep, give = part(place, 3, 2, keep, got)
    pieces = part(place, 4, chips // 2, keep, swap(give, "band", bands_total, 2))
    total = pieces[0]
    for d in range(1, chips // 2):
        total = total + swap(pieces[d], "band", bands_total, 4 * d)

    total = jnp.stack([total, swap(total, "band", bands_total, 1)])
    total = jnp.stack([total, swap(total, "band", bands_total, 2)])
    final = [total] + [swap(total, "band", bands_total, 4 * d) for d in range(1, chips // 2)]
    return settle(place, final, energy_count, states // pw_total, states)


def solution(mesh):
    bands_total, pw_total = mesh.shape["band"], mesh.shape["pw"]

    def body(*args):
        return local(bands_total, pw_total, CHUNKS, *args)

    return jax.shard_map(
        body,
        mesh=mesh,
        in_specs=(
            P("band", None, "pw"),
            P("pw", "band"),
            P("pw", "band"),
            P("band"),
            P("band"),
            P(),
            P(),
        ),
        out_specs=P(None, "pw", None),
        check_vma=False,
    )
```
